512 devices in a mesh: col: 64 (over z, y), row: 8 (over x, core).
Axes of the slice: x: 4, y: 4, z: 16, core: 2. Of those that a mesh axis runs over, the one named last changes fastest.
Arguments:
- static_flex: float32 [8192, 32768], P('row', 'col'), may hold values from -6 to 6
- phi_slab: float32 [8192, 1024], P('row', 'col'), may hold values from -6 to 6
- phi_cols: float32 [32768, 1024], P('col', 'row'), may hold values from -6 to 6
- eigenvalues: float32 [1024], P('col'), may hold values from 8 to 128
Outputs:
- residual_flex: float32 [8192, 32768], P('row', 'col')
The draws below stay inside these ranges and needn't reach their ends.
All inputs are finite; a program needn't handle non-finite values.
Results may differ from the reference program's by a relative error of at most 0.00005.
Values sent between devices are 32-bit elements; how exact they have to be, the bound alone decides.
A program may use at most 64 MiB of HBM per device.

```python
import math
import jax
import jax.numpy as jnp
from jax import lax

MODES = 1024
BOUNDARY = 32768
SLAB = 8192


def level_of(own_key, shape, shards, least, high):
    loudness, own = 1.0, jax.random.fold_in(own_key, 6)
    for dim, shards_of in shards:
        steps = jnp.exp(jax.random.uniform(jax.random.fold_in(own, dim), (shards_of,), jnp.float32, least / len(shards), high / len(shards)))
        loudness = loudness * jnp.repeat(steps, shape[dim] // shards_of).reshape([-1 if axis == dim else 1 for axis in range(len(shape))])
    return loudness


def normal_values(rng, dims, deviation, limit, split=(), kind=jnp.bfloat16):
    gain = level_of(rng, dims, split, -0.22, 0.18) if split else 1.0
    result = jax.random.normal(rng, dims, jnp.float32) * deviation * gain
    return jnp.minimum(jnp.maximum(result, -limit), limit).astype(kind)


def setup_inputs(seed: int = 0) -> dict:
    arg_keys = jax.random.split(jax.random.key(seed), 5)
    static_flex = normal_values(arg_keys[0], (SLAB, BOUNDARY), 1.0, 6.0, ((0, 8), (1, 64)), jnp.float32)
    phi_slab = normal_values(arg_keys[1], (SLAB, MODES), 1.0, 6.0, ((0, 8), (1, 64)), jnp.float32)
    phi_cols = normal_values(arg_keys[2], (BOUNDARY, MODES), 1.0, 6.0, ((0, 64), (1, 8)), jnp.float32)
    eigenvalues = jnp.clip(jnp.exp(math.log(128.0) - 2.7725887 * jax.random.uniform(arg_keys[3], (MODES,), jnp.float32) ** level_of(arg_keys[3], (MODES,), ((0, 64),), -0.2, 0.2)), 8.0, 128.0)
    return {"static_flex": static_flex, "phi_slab": phi_slab, "phi_cols": phi_cols, "eigenvalues": eigenvalues}


def reference(static_flex, phi_slab, phi_cols, eigenvalues):
    scaled = phi_slab / eigenvalues[None, :]
    update = lax.dot_general(scaled, phi_cols, (((1,), (1,)), ((), ())), precision=lax.Precision.HIGHEST, preferred_element_type=jnp.float32)
    return static_flex - update
```

```python
import functools

import jax
import jax.numpy as jnp
from jax import lax
from jax.experimental import pallas as pl
from jax.experimental.pallas import tpu as pltpu
from jax.sharding import PartitionSpec as P

MESH = pl.DeviceIdType.MESH
NZ, NY, NX = 16, 4, 4
CUT = 384
TILE = 256


def plan_names():
    names = []
    for sign in (1, -1):
        for d in range(1, 9):
            names.append(("Qz", sign, d))
            for dy in range(NY):
                names.append(("Pz", sign, d, dy))
        names.append(("Py", sign))
        names.append(("Py2", sign))
        for e in range(-7, 9):
            names.append(("Qy", e, sign))
            names.append(("Qy2", e, sign))
        names.append(("Bx", sign))
        names.append(("Bx2", sign))
        names.append(("Bc", sign))
        names.append(("Bc2", sign))
    names.append(("Bc0",))
    return {name: number for number, name in enumerate(names)}


NAMES = plan_names()


def kernel(eig, slab, cols, out, raw, at, ball, bh, bl, send_sem, recv_sem, local_sem):
    col, row = lax.axis_index("col"), lax.axis_index("row")
    z, y = col // NY, col % NY
    x, core = row // 2, row % 2
    modes, lanes = slab.shape
    half = modes // 2
    n = cols.shape[0]

    def mod(value, size):
        return lax.rem(value + 2 * size, size)

    def at_z(step):
        return {"col": mod(z + step, NZ) * NY + y}

    def at_y(step):
        return {"col": z * NY + mod(y + step, NY)}

    def at_x(step):
        return {"row": mod(x + step, NX) * 2 + core}

    partner = {"row": x * 2 + (1 - core)}

    def copy(name, ref, device):
        number = NAMES[name]
        return pltpu.make_async_remote_copy(
            src_ref=ref,
            dst_ref=ref,
            send_sem=send_sem.at[number],
            recv_sem=recv_sem.at[number],
            device_id=device,
            device_id_type=MESH,
        )

    sent = []

    def send(name, ref, device):
        move = copy(name, ref, device)
        move.start()
        sent.append(move)

    def arrive(name, ref):
        copy(name, ref, partner).wait_recv()

    def part(e, dy, which, rows=None):
        lane = pl.ds(0, CUT) if which == "P" else pl.ds(CUT, lanes - CUT)
        sub = pl.ds(0, modes) if rows is None else pl.ds(rows * half, half)
        return at.at[mod(z - e, NZ), mod(y - dy, NY), sub, lane]

    def half_of(sign):
        return 0 if sign > 0 else 1

    def block(dx, c, rows=None):
        sub = pl.ds(0, n) if rows is None else pl.ds(rows * (n // 2), n // 2)
        return ball.at[mod(x - dx, NX) * 2 + c, sub, :]

    load_slab = pltpu.make_async_copy(slab, raw, local_sem.at[0])
    load_cols = pltpu.make_async_copy(cols, ball.at[row], local_sem.at[1])
    load_slab.start()
    load_cols.start()
    barrier = pltpu.get_barrier_semaphore()
    for device in (at_z(1), at_z(-1), at_y(1), at_y(-1), at_x(1), at_x(-1), partner):
        pl.semaphore_signal(barrier, inc=1, device_id=device, device_id_type=MESH)
    load_slab.wait()
    index = lax.broadcasted_iota(jnp.int32, (modes, 128), 0)
    scale = jnp.zeros((modes, 128), jnp.float32)
    for k in range(modes):
        scale = jnp.where(index == k, eig[k], scale)
    for lane in range(0, lanes, 128):
        at[z, y, :, pl.ds(lane, 128)] = raw[:, pl.ds(lane, 128)] / scale
    load_cols.wait()
    pl.semaphore_wait(barrier, 7)

    for sign in (1, -1):
        send(("Qz", sign, 1), part(0, 0, "Q"), at_z(sign))
        send(("Py", sign), part(0, 0, "P"), at_y(sign))
    for sign in (1, -1):
        send(("Bx", sign), block(0, core), at_x(sign))
        send(("Pz", sign, 1, 0), part(0, 0, "P"), at_z(sign))
        send(("Qy", 0, sign), part(0, 0, "Q"), at_y(sign))
    send(("Bc0",), block(0, core), partner)

    def q_z(s):
        for sign in (1, -1):
            if s < 8:
                arrive(("Qz", sign, s), part(sign * s, 0, "Q"))
                rows = None if s < 7 else half_of(sign)
                send(("Qz", sign, s + 1), part(sign * s, 0, "Q", rows), at_z(sign))
            else:
                arrive(("Qz", sign, s), part(8, 0, "Q", half_of(sign)))
        for e in (s, -s) if s < 8 else (8,):
            for sign in (1, -1):
                send(("Qy", e, sign), part(e, 0, "Q"), at_y(sign))

    def q_y(s):
        for e in (s, -s) if 0 < s < 8 else (s,):
            for sign in (1, -1):
                arrive(("Qy", e, sign), part(e, sign, "Q"))
                send(("Qy2", e, sign), part(e, sign, "Q", half_of(sign)), at_y(sign))

    def q_y2(s):
        for e in (s, -s) if 0 < s < 8 else (s,):
            for sign in (1, -1):
                arrive(("Qy2", e, sign), part(e, 2, "Q", half_of(sign)))

    def p_z(s):
        for dy in (0, 1, -1, 2):
            for sign in (1, -1):
                if s < 8:
                    arrive(("Pz", sign, s, dy % NY), part(sign * s, dy, "P"))
                    rows = None if s < 7 else half_of(sign)
                    send(("Pz", sign, s + 1, dy % NY), part(sign * s, dy, "P", rows), at_z(sign))
                else:
                    arrive(("Pz", sign, s, dy % NY), part(8, dy, "P", half_of(sign)))

    def p_y():
        for sign in (1, -1):
            arrive(("Py", sign), part(0, sign, "P"))
            send(("Py2", sign), part(0, sign, "P", half_of(sign)), at_y(sign))
        for sign in (1, -1):
            for way in (1, -1):
                send(("Pz", way, 1, sign % NY), part(0, sign, "P"), at_z(way))

    def p_y2():
        for sign in (1, -1):
            arrive(("Py2", sign), part(0, 2, "P", half_of(sign)))
        for way in (1, -1):
            send(("Pz", way, 1, 2), part(0, 2, "P"), at_z(way))

    def b_x():
        for sign in (1, -1):
            arrive(("Bx", sign), block(sign, core))
            send(("Bx2", sign), block(sign, core, half_of(sign)), at_x(sign))
            send(("Bc", sign), block(sign, core), partner)

    def b_x2():
        for sign in (1, -1):
            arrive(("Bx2", sign), block(2, core, half_of(sign)))
            send(("Bc2", sign), block(2, core, half_of(sign)), partner)

    def b_c():
        arrive(("Bc0",), block(0, 1 - core))
        for sign in (1, -1):
            arrive(("Bc", sign), block(sign, 1 - core))
            arrive(("Bc2", sign), block(2, 1 - core, half_of(sign)))

        @pl.loop(0, 8)
        def _(r):
            value = ball[r]
            high = value.astype(jnp.bfloat16)
            bh[r] = high
            bl[r] = (value - high.astype(jnp.float32)).astype(jnp.bfloat16)

    groups = modes * NY * 2
    pair = mod(z // 2, NZ // 2)

    def compute(offsets, first=False):
        picks = [mod(pair + offset, NZ // 2) for offset in offsets]

        @pl.loop(0, lanes // TILE)
        def _(tile):
            sub = pl.ds(pl.multiple_of(tile * TILE, TILE), TILE)
            left = []
            for pick in picks:
                left.append(at[pl.ds(pick * 2, 2), :, :, sub].reshape(groups, TILE).T)
            left = jnp.concatenate(left, axis=1) if len(left) > 1 else left[0]
            high = left.astype(jnp.bfloat16)
            low = (left - high.astype(jnp.float32)).astype(jnp.bfloat16)
            right_high = [bh[pick] for pick in picks]
            right_low = [bl[pick] for pick in picks]
            lhs = jnp.concatenate([high, high, low], axis=1)
            rhs = jnp.concatenate(right_high + right_low + right_high, axis=1)
            total = lax.dot_general(lhs, rhs, (((1,), (1,)), ((), ())), preferred_element_type=jnp.float32)
            if first:
                out[sub, :] = total
            else:
                out[sub, :] += total

    q_z(1)
    p_y()
    b_x()
    q_y(0)
    p_y2()
    q_z(2)
    p_z(1)
    q_y(1)
    b_x2()
    q_z(3)
    p_z(2)
    q_y(2)
    q_z(4)
    p_z(3)
    q_y(3)
    b_c()
    q_y2(0)
    q_y2(1)
    compute((0,), first=True)
    q_z(5)
    p_z(4)
    q_y(4)
    q_y2(2)
    q_y2(3)
    compute((-1, 1))
    q_z(6)
    p_z(5)
    q_y(5)
    q_z(7)
    p_z(6)
    q_y(6)
    q_y2(4)
    q_y2(5)
    compute((-2, 2))
    q_z(8)
    p_z(7)
    q_y(7)
    q_y2(6)
    q_y(8)
    q_y2(7)
    compute((-3, 3))
    p_z(8)
    q_y2(8)
    compute((4,))
    for move in sent:
        move.wait_send()


def local(static_flex, phi_slab, phi_cols, eigenvalues):
    modes, lanes = phi_slab.shape[1], phi_slab.shape[0]
    n, depth = phi_cols.shape
    count = len(NAMES)
    update = pl.pallas_call(
        kernel,
        out_shape=jax.ShapeDtypeStruct((lanes, n), jnp.float32),
        in_specs=[
            pl.BlockSpec(memory_space=pltpu.SMEM),
            pl.BlockSpec(memory_space=pl.ANY),
            pl.BlockSpec(memory_space=pl.ANY),
        ],
        out_specs=pl.BlockSpec(memory_space=pltpu.VMEM),
        scratch_shapes=[
            pltpu.VMEM((modes, lanes), jnp.float32),
            pltpu.VMEM((NZ, NY, modes, lanes), jnp.float32),
            pltpu.VMEM((8, n, depth), jnp.float32),
            pltpu.VMEM((8, n, depth), jnp.bfloat16),
            pltpu.VMEM((8, n, depth), jnp.bfloat16),
            pltpu.SemaphoreType.DMA((count,)),
            pltpu.SemaphoreType.DMA((count,)),
            pltpu.SemaphoreType.DMA((2,)),
        ],
        compiler_params=pltpu.CompilerParams(
            collective_id=0, has_side_effects=True, vmem_limit_bytes=32 * 2**20
        ),
        cost_estimate=pl.CostEstimate(flops=3 * 2**30, bytes_accessed=8 * 2**20, transcendentals=0),
        name="gather_update",
    )(eigenvalues, phi_slab.T, phi_cols)
    return static_flex - update


def solution(mesh):
    placed = (P("row", "col"), P("row", "col"), P("col", "row"), P("col"))
    return jax.shard_map(local, mesh=mesh, in_specs=placed, out_specs=P("row", "col"), check_vma=False)
```
